32 devices in a mesh: ord: 8 (over z, core), gx: 2 (over x), gy: 2 (over y).
Axes of the slice: x: 2, y: 2, z: 4, core: 2. Of those that a mesh axis runs over, the one named last changes fastest.
Arguments:
- distribution: float32 [256, 64, 8, 128], P('ord', 'gx', 'gy'), may hold values from -4.5 to 4.5
- relaxation: float32 [64, 8, 128], P('gx', 'gy'), may hold values from 0.05 to 5
Outputs:
- updated: float32 [256, 64, 8, 128], P('ord', 'gx', 'gy')
- temperature: float32 [64, 8, 128], P('gx', 'gy')
The draws below stay inside these ranges and needn't reach their ends.
All inputs are finite; a program needn't handle non-finite values.
Results may differ from the reference program's by a relative error of at most 0.0003.
Values sent between devices are 32-bit elements; how exact they have to be, the bound alone decides.
A program may use at most 64 MiB of HBM per device.

```python
import math
import jax
import jax.numpy as jnp
from jax import lax

NORD = 256
STEPS = 2
SWEEPS = 3
NX = 64
NY = 8
NZ = 128


def draw_distribution(key, part):
    base_key = jax.random.fold_in(key, 71)
    spread_key = jax.random.fold_in(key, 72)
    base = jnp.clip(jax.random.normal(base_key, (NX, NY, NZ), jnp.float32), -3.0, 3.0)
    aside = 0.5 * jnp.clip(jax.random.normal(spread_key, (NORD, NX, NY, NZ), jnp.float32), -3.0, 3.0)
    return base[None] + aside


def block_scale(key, extent, cuts, least, high):
    gain, own = 1.0, jax.random.fold_in(key, 6)
    for dim, blocks in cuts:
        steps = jnp.exp(jax.random.uniform(jax.random.fold_in(own, dim), (blocks,), jnp.float32, least / len(cuts), high / len(cuts)))
        gain = gain * jnp.repeat(steps, extent[dim] // blocks).reshape([-1 if axis == dim else 1 for axis in range(len(extent))])
    return gain


def setup_inputs(seed: int = 0) -> dict:
    streams_of = jax.random.split(jax.random.key(seed), 3)
    distribution = draw_distribution(jax.random.fold_in(streams_of[2], 71), 0)
    relaxation = jnp.clip(jnp.exp(math.log(5.0) - 4.6051702 * jax.random.uniform(streams_of[1], (NX, NY, NZ), jnp.float32) ** block_scale(streams_of[1], (NX, NY, NZ), ((0, 2), (1, 2)), -0.2, 0.2)), 0.05, 5.0)
    return dict(distribution=distribution, relaxation=relaxation)


time_step = 0.4
limiter_eps = 0.01
diffusion_mass = 0.5
flux_weight = 2.0
golden_turn = 2.399963229728653
ordinate_block = 8

def directions(offset, length):
    ordinal = (offset + jnp.arange(length, dtype=jnp.int32)).astype(jnp.float32)
    height = 1.0 - (2.0 * ordinal + 1.0) / NORD
    radius = jnp.sqrt(1.0 - height * height)
    turned = golden_turn * ordinal
    return jnp.stack([radius * jnp.cos(turned), radius * jnp.sin(turned), height])

def window(values, anchor, length, axis_dim):
    return lax.slice_in_dim(values, anchor, anchor + length, axis=axis_dim)

def pad_along(values, width, axis_dim):
    widths = [(width, width) if dimension == axis_dim else (0, 0) for dimension in range(values.ndim)]
    return jnp.pad(values, widths)

def source_of(current, local_temp, relax):
    return ((2.0 * relax - time_step) * current + 2.0 * time_step * local_temp) / (2.0 * relax + time_step)

def axis_flux(padded, temp_pad, relax_pad, along_speed, axis_dim):
    length = padded.shape[axis_dim] - 4
    lower_diff = window(padded, 1, length + 2, axis_dim) - window(padded, 0, length + 2, axis_dim)
    upper_diff = window(padded, 2, length + 2, axis_dim) - window(padded, 1, length + 2, axis_dim)
    centre = window(padded, 1, length + 2, axis_dim)
    slopes = (lower_diff * (upper_diff * upper_diff + limiter_eps) + upper_diff * (lower_diff * lower_diff + limiter_eps)) / (lower_diff * lower_diff + upper_diff * upper_diff + 2.0 * limiter_eps)
    upwind_low = window(centre, 0, length + 1, axis_dim) + 0.5 * (1.0 - time_step * along_speed) * window(slopes, 0, length + 1, axis_dim)
    upwind_high = window(centre, 1, length + 1, axis_dim) - 0.5 * (1.0 + time_step * along_speed) * window(slopes, 1, length + 1, axis_dim)
    upwind = jnp.where(along_speed >= 0.0, upwind_low, upwind_high)
    temp_face = 0.5 * (window(temp_pad, 0, length + 1, axis_dim) + window(temp_pad, 1, length + 1, axis_dim))
    relax_face = 0.5 * (window(relax_pad, 0, length + 1, axis_dim) + window(relax_pad, 1, length + 1, axis_dim))
    edges = (2.0 * relax_face * upwind + 0.5 * time_step * temp_face) / (2.0 * relax_face + 0.5 * time_step)
    return along_speed * (window(edges, 1, length, axis_dim) - window(edges, 0, length, axis_dim))

def spread(flux_x_pad, flux_y_pad, flux_z):
    flux_z_pad = jnp.pad(flux_z, ((0, 0), (0, 0), (1, 1)))
    result = 0.5 * (flux_x_pad[2:, 1:-1, 1:-1] - flux_x_pad[:-2, 1:-1, 1:-1])
    result = result + 0.5 * (flux_y_pad[1:-1, 2:, 1:-1] - flux_y_pad[1:-1, :-2, 1:-1])
    return result + 0.5 * (flux_z_pad[:, :, 2:] - flux_z_pad[:, :, :-2])

def relax_sweep(potential_pad, driver):
    conduct = 1.0 / (1.0 + potential_pad * potential_pad)
    centre = conduct[1:-1, 1:-1, 1:-1]
    weighted = diffusion_mass * driver
    weights = diffusion_mass + jnp.zeros_like(driver)
    for axis_dim in range(3):
        for anchor in (0, 2):
            picker = tuple((slice(anchor, anchor + potential_pad.shape[axis_dim] - 2) if dimension == axis_dim else slice(1, -1) for dimension in range(3)))
            couple = 0.5 * (centre + conduct[picker])
            weighted = weighted + couple * potential_pad[picker]
            weights = weights + couple
    return weighted / weights

def advance(block, speed_block, local_temp, relax):
    source = source_of(block, local_temp, relax)
    fluxes = jnp.zeros_like(source)
    for axis_dim in (1, 2, 3):
        fluxes = fluxes + axis_flux(pad_along(source, 2, axis_dim), pad_along(local_temp[None], 1, axis_dim), pad_along(relax[None], 1, axis_dim), speed_block[axis_dim - 1][:, None, None, None], axis_dim)
    return source - time_step * fluxes

def reference(distribution, relaxation):
    speeds = directions(0, NORD)
    groups = NORD // ordinate_block
    grouped_speeds = speeds.reshape(3, groups, ordinate_block).transpose(1, 0, 2)
    current = distribution
    for repeat in range(STEPS):
        local_temp = lax.optimization_barrier(jnp.sum(current, 0)) / NORD
        blocks = current.reshape(groups, ordinate_block, NX, NY, NZ)
        advanced = lax.map(lambda operands: advance(operands[0], operands[1], local_temp, relaxation), (blocks, grouped_speeds))
        current = advanced.reshape(NORD, NX, NY, NZ)
    energy = lax.optimization_barrier(jnp.sum(current, 0)) / NORD
    fluxes = jnp.tensordot(speeds, current, axes=(1, 0), precision=lax.Precision.HIGHEST) / NORD
    padded = jnp.pad(jnp.stack([fluxes[0], fluxes[1]]), ((0, 0), (1, 1), (1, 1), (1, 1)))
    driver = energy - flux_weight * spread(padded[0], padded[1], fluxes[2])
    potential = energy
    for rounds in range(SWEEPS):
        potential = relax_sweep(jnp.pad(potential, 1), driver)
    updated = source_of(current, potential, relaxation)
    return (updated, potential)
```

```python
import jax
import jax.numpy as jnp
from jax import lax
from jax.experimental import pallas as pl
from jax.experimental.pallas import tpu as pltpu
from jax.sharding import PartitionSpec as P

NORD = 256
STEPS = 2
SWEEPS = 3
LANE_GROUP = 8

h = 0.4
eps = 0.01
diffusion_mass = 0.5
flux_weight = 2.0
golden_turn = 2.399963229728653
MESH = pl.DeviceIdType.MESH
f32 = jnp.float32


def directions(offset, length):
    ordinal = (offset + jnp.arange(length, dtype=jnp.int32)).astype(jnp.float32)
    height = 1.0 - (2.0 * ordinal + 1.0) / NORD
    radius = jnp.sqrt(1.0 - height * height)
    turned = golden_turn * ordinal
    return jnp.stack([radius * jnp.cos(turned), radius * jnp.sin(turned), height])


def slope_of(a, b, aa, bb):
    return (a + b) * (a * b + eps) / (aa + bb)


def kernel(dims, speed, dist, relax, out, temp_out, *scratch):
    NO, NX, NY, O, X, Y, Z = dims
    (q0, q1, q2, src, hx, hy, acc, tmix, te, re, pe, fxe, fye, drv, px, qx, py, qy, pzh, pzl, dqz,
     ca, cb, part, rbuf, full, ssx, ssy, hsx, hsy, b_send, b_recv, s_send, s_recv, p_send, p_recv) = scratch
    G = O // LANE_GROUP
    N = X * Y
    R = N // NO
    U = LANE_GROUP
    XO = 8
    mo, mx, my = lax.axis_index("ord"), lax.axis_index("gx"), lax.axis_index("gy")
    has = (mx > 0, mx < NX - 1, my > 0, my < NY - 1)
    peer = ({"gx": mx - 1}, {"gx": mx + 1}, {"gy": my - 1}, {"gy": my + 1})

    barrier = pltpu.get_barrier_semaphore()
    for k in range(1, NO):
        pl.semaphore_signal(barrier, inc=1, device_id={"ord": lax.rem(mo + k, NO)}, device_id_type=MESH)
    for side in range(4):
        @pl.when(has[side])
        def _():
            pl.semaphore_signal(barrier, inc=1, device_id=peer[side], device_id_type=MESH)
    ends = sum((jnp.where(flag, 1, 0) for flag in has), 0)
    pl.semaphore_wait(barrier, NO - 1 + ends)

    def small_copy(ev, layers, side):
        buf_s, buf_r = (ssx, hsx) if side < 2 else (ssy, hsy)
        mine, theirs = side % 2, 1 - side % 2
        return pltpu.make_async_remote_copy(
            src_ref=buf_s.at[ev, mine, pl.ds(0, layers)],
            dst_ref=buf_r.at[ev, theirs, pl.ds(0, layers)],
            send_sem=s_send.at[ev, side],
            recv_sem=s_recv.at[ev, side ^ 1],
            device_id=peer[side], device_id_type=MESH)

    def small_recv(ev, layers, side):
        buf_s, buf_r = (ssx, hsx) if side < 2 else (ssy, hsy)
        return pltpu.make_async_remote_copy(
            src_ref=buf_s.at[ev, side % 2, pl.ds(0, layers)],
            dst_ref=buf_r.at[ev, side % 2, pl.ds(0, layers)],
            send_sem=s_send.at[ev, side],
            recv_sem=s_recv.at[ev, side],
            device_id=peer[side], device_id_type=MESH)

    def small_start(ev, layers, fx, fy):
        for l in range(layers):
            for y in range(Y):
                ssx[ev, 0, l, y:y + 1, :] = fx[y + 2, XO + l:XO + l + 1, :]
                ssx[ev, 1, l, y:y + 1, :] = fx[y + 2, XO + X - layers + l:XO + X - layers + l + 1, :]
            ssy[ev, 0, l] = fy[2 + l, XO:XO + X, :]
            ssy[ev, 1, l] = fy[2 + Y - layers + l, XO:XO + X, :]
        for side in range(4):
            @pl.when(has[side])
            def _():
                small_copy(ev, layers, side).start()

    def small_finish(ev, layers, fx, fy):
        for side in range(4):
            @pl.when(has[side])
            def _():
                small_recv(ev, layers, side).wait_recv()
                for l in range(layers):
                    if side < 2:
                        at = XO - layers + l if side == 0 else XO + X + l
                        for y in range(Y):
                            fx[y + 2, at:at + 1, :] = hsx[ev, side % 2, l, y:y + 1, :]
                    else:
                        at = 2 - layers + l if side == 2 else 2 + Y + l
                        fy[at, XO:XO + X, :] = hsy[ev, side % 2, l]

    bigs = (q0, q1)

    def big(t, g, side, sending):
        q = bigs[t]
        if side < 2:
            lo = 0 if side == 0 else X - 2
            s = q.at[g, :, pl.ds(lo, 2)]
            buf = hx
        else:
            lo = 0 if side == 2 else Y - 2
            s = q.at[g, pl.ds(lo, 2)]
            buf = hy
        slot = (1 - side % 2) if sending else side % 2
        return pltpu.make_async_remote_copy(
            src_ref=s, dst_ref=buf.at[t, slot, g],
            send_sem=b_send.at[t, g, side],
            recv_sem=b_recv.at[t, g, side ^ 1 if sending else side],
            device_id=peer[side], device_id_type=MESH)

    def psum_scatter_copy(ev, fields, k):
        to = lax.rem(mo + k, NO)
        return pltpu.make_async_remote_copy(
            src_ref=part.at[ev, to, pl.ds(0, fields)], dst_ref=rbuf.at[ev, k, pl.ds(0, fields)],
            send_sem=p_send.at[ev, 0, k], recv_sem=p_recv.at[ev, 0, k],
            device_id={"ord": to}, device_id_type=MESH)

    def psum_gather_copy(ev, fields, k, owner):
        to = lax.rem(mo + k, NO)
        return pltpu.make_async_remote_copy(
            src_ref=full.at[ev, mo, pl.ds(0, fields)], dst_ref=full.at[ev, owner, pl.ds(0, fields)],
            send_sem=p_send.at[ev, 1, k], recv_sem=p_recv.at[ev, 1, k],
            device_id={"ord": to}, device_id_type=MESH)

    def psum_start(ev, fields):
        for k in range(1, NO):
            psum_scatter_copy(ev, fields, k).start()

    def psum_finish(ev, fields):
        for k in range(1, NO):
            psum_scatter_copy(ev, fields, k).wait_recv()
        for f in range(fields):
            total = part[ev, mo, f]
            for k in range(1, NO):
                total = total + rbuf[ev, k, f]
            full[ev, mo, f] = total * (1.0 / NORD)
        for k in range(1, NO):
            psum_gather_copy(ev, fields, k, mo).start()
        for k in range(1, NO):
            psum_gather_copy(ev, fields, k, lax.rem(mo + NO - k, NO)).wait_recv()

    def rows(r):
        return r // R, r % R

    def unpack(ev, f, dst):
        for y in range(Y):
            for n in range(max(1, X // R)):
                size = min(R, X)
                r0 = y * X + n * size
                dst[y + 2, XO + n * size:XO + (n + 1) * size, :] = full[ev, r0 // R, f, r0 % R:r0 % R + size, :]

    def put_plane(ev, f, y, value):
        size = min(R, X)
        for n in range(X // size):
            r0 = y * X + n * size
            part[ev, r0 // R, f, r0 % R:r0 % R + size, :] = value[n * size:(n + 1) * size]

    for ref in (te, re, pe, fxe, fye):
        ref[...] = jnp.zeros_like(ref)
    for y in range(Y):
        re[y + 2, XO:XO + X, :] = relax[pl.ds(y, X, stride=Y), :]
    small_start(0, 2, re, re)

    @pl.loop(0, G)
    def _(g):
        @pl.loop(0, X)
        def _(x):
            for y in range(Y):
                q0[g, y, x] = dist[pl.ds(g * U * N + x * Y + y, U, stride=N), :]
        for side in range(4):
            @pl.when(has[side])
            def _():
                big(0, g, side, True).start()

    @pl.loop(0, N // 8)
    def _(i):
        at = pl.multiple_of(i * 8, 8)
        total = dist[pl.ds(at, 8), :]
        for o in range(1, O):
            total = total + dist[pl.ds(o * N + at, 8), :]
        tmix[pl.ds(at, 8), :] = total
    for y in range(Y):
        put_plane(0, 0, y, tmix[pl.ds(y, X, stride=Y), :])
    psum_start(0, 1)

    src[...] = jnp.zeros_like(src)
    small_finish(0, 2, re, re)
    lane = lax.broadcasted_iota(jnp.int32, (X, Z), 1)

    def shift_up(v):
        return jnp.where(lane == Z - 1, 0.0, pltpu.roll(v, Z - 1, 1))

    def shift_down(v):
        return jnp.where(lane == 0, 0.0, pltpu.roll(v, 1, 1))

    XA = X + 2 * XO

    def face_r(r0, r1):
        r = 0.5 * (r0 + r1)
        return 2.0 * r / (2.0 * r + 0.5 * h)

    def face_t(t0, t1, p):
        return 0.5 * (t0 + t1) * (1.0 - p)

    for y in range(Y + 4):
        r = re[y]
        ca[y] = (2.0 * r - h) / (2.0 * r + h)
    for y in range(Y):
        r = re[y + 2, XO:XO + X, :]
        px[y, 0:X, :] = face_r(re[y + 2, XO - 1:XO - 1 + X, :], r)
        px[y, X:X + 1, :] = face_r(re[y + 2, XO + X - 1:XO + X, :], re[y + 2, XO + X:XO + X + 1, :])
        pzh[y] = face_r(r, shift_up(r))
        pzl[y] = face_r(shift_down(r), r)
    for y in range(Y + 1):
        py[y] = face_r(re[y + 1, XO:XO + X, :], re[y + 2, XO:XO + X, :])

    def coefficients():
        for y in range(Y + 4):
            cb[y] = 2.0 * h * te[y] / (2.0 * re[y] + h)
        for y in range(Y):
            t = te[y + 2, XO:XO + X, :]
            qx[y, 0:X, :] = face_t(te[y + 2, XO - 1:XO - 1 + X, :], t, px[y, 0:X, :])
            qx[y, X:X + 1, :] = face_t(te[y + 2, XO + X - 1:XO + X, :], te[y + 2, XO + X:XO + X + 1, :], px[y, X:X + 1, :])
            dqz[y] = face_t(t, shift_up(t), pzh[y]) - face_t(shift_down(t), t, pzl[y])
        for y in range(Y + 1):
            qy[y] = face_t(te[y + 1, XO:XO + X, :], te[y + 2, XO:XO + X, :], py[y])

    def row(ref, y, x):
        return jnp.broadcast_to(ref[y, pl.ds(x, 1), :], (U, Z))

    lane8 = lax.broadcasted_iota(jnp.int32, (U, Z), 1)

    def advance(t, g):
        q, qn = (q0, q1, q2)[t], (q0, q1, q2)[t + 1]

        @pl.loop(0, X)
        def _(x):
            for y in range(Y):
                src[y + 2, x + 2] = row(ca, y + 2, XO + x) * q[g, y, x] + row(cb, y + 2, XO + x)
        for side in range(4):
            @pl.when(has[side])
            def _():
                big(t, g, side, False).wait_recv()
                if side < 2:
                    for l in range(2):
                        x = (l - 2) if side == 0 else X + l
                        for y in range(Y):
                            src[y + 2, x + 2] = row(ca, y + 2, XO + x) * hx[t, side, g, y, l] + row(cb, y + 2, XO + x)
                else:
                    @pl.loop(0, X)
                    def _(x):
                        for l in range(2):
                            y = (l - 2) if side == 2 else Y + l
                            src[y + 2, x + 2] = row(ca, y + 2, XO + x) * hy[t, side - 2, g, l, x] + row(cb, y + 2, XO + x)

        cx, cy, cz = speed[0, g], speed[1, g], speed[2, g]

        def gamma(c):
            return jnp.where(c >= 0.0, 0.5 * (1.0 - h * c), -0.5 * (1.0 + h * c))

        gx_, gy_, gz_ = gamma(cx), gamma(cy), gamma(cz)
        gz_abs = jnp.abs(gz_)
        hcx, hcy, hcz = h * cx, h * cy, h * cz

        start = []
        for y in range(Y):
            sm2, sm1, s0, s1 = (src[y + 2, i] for i in range(4))
            a, b, c = sm1 - sm2, s0 - sm1, s1 - s0
            aa, bb, cc = a * a + eps, b * b + eps, c * c + eps
            um = sm1 + gx_ * slope_of(a, b, aa, bb)
            u0 = s0 + gx_ * slope_of(b, c, bb, cc)
            e0 = row(px, y, 0) * jnp.where(cx >= 0.0, um, u0) + row(qx, y, 0)
            start += [u0, e0, c]

        def body(x, carry):
            posx, posy, posz = cx >= 0.0, cy >= 0.0, cz >= 0.0
            column = [src[j, x + 2] for j in range(Y + 4)]
            d = [column[j + 1] - column[j] for j in range(Y + 3)]
            e = [v * v + eps for v in d]
            u = [None] + [column[j] + gy_ * slope_of(d[j - 1], d[j], e[j - 1], e[j]) for j in range(1, Y + 3)]
            ey = [row(py, f, x) * jnp.where(posy, u[f + 1], u[f + 2]) + row(qy, f, x) for f in range(Y + 1)]
            carried = []
            for y in range(Y):
                s = column[y + 2]
                u0, e0, c = carry[3 * y:3 * y + 3]
                s1, s2 = src[y + 2, x + 3], src[y + 2, x + 4]
                d1 = s2 - s1
                u1 = s1 + gx_ * slope_of(c, d1, c * c + eps, d1 * d1 + eps)
                e1 = row(px, y, x + 1) * jnp.where(posx, u0, u1) + row(qx, y, x + 1)
                carried += [u1, e1, d1]
                za = s - jnp.where(lane8 == 0, 0.0, pltpu.roll(s, 1, 1))
                zb = jnp.where(lane8 == Z - 1, 0.0, pltpu.roll(s, Z - 1, 1)) - s
                uz = s + gz_ * slope_of(za, zb, za * za + eps, zb * zb + eps)
                ghost = gz_abs * (s * eps / (s * s + 2.0 * eps))
                wl = jnp.where(lane8 == 0, ghost, pltpu.roll(uz, 1, 1))
                wr = jnp.where(lane8 == Z - 1, ghost, pltpu.roll(uz, Z - 1, 1))
                up_hi = jnp.where(posz, uz, wr)
                up_lo = jnp.where(posz, wl, uz)
                fz = row(pzh, y, x) * up_hi - row(pzl, y, x) * up_lo + row(dqz, y, x)
                new = s - (hcx * (e1 - e0) + hcy * (ey[y + 1] - ey[y]) + hcz * fz)
                qn[g, y, x] = new
                if t == 0:
                    acc[0, y, x] += new
                else:
                    acc[0, y, x] += new
                    acc[1, y, x] += cx * new
                    acc[2, y, x] += cy * new
                    acc[3, y, x] += cz * new
            return tuple(carried)

        lax.fori_loop(0, X, body, tuple(start))

    def fold(f, y, dst):
        @pl.loop(0, X)
        def _(x):
            dst[y, pl.ds(XO + x, 1), :] = jnp.sum(acc[f, y, x], axis=0, keepdims=True)

    for t in range(STEPS):
        psum_finish(t, 1)
        unpack(t, 0, te)
        small_start(1 + t, 2, te, te)
        acc[...] = jnp.zeros_like(acc)
        small_finish(1 + t, 2, te, te)
        coefficients()

        @pl.loop(0, G)
        def _(g):
            advance(t, g)
            if t + 1 < STEPS:
                for side in range(4):
                    @pl.when(has[side])
                    def _():
                        big(t + 1, g, side, True).start()

        if t + 1 < STEPS:
            for y in range(Y):
                fold(0, y, drv)
                put_plane(t + 1, 0, y, drv[y, XO:XO + X, :])
            psum_start(t + 1, 1)

    for y in range(Y):
        for f, dst, at in ((1, fxe, y + 2), (2, fye, y + 2), (0, te, y), (3, drv, y)):
            @pl.loop(0, X)
            def _(x):
                dst[at, pl.ds(XO + x, 1), :] = jnp.sum(acc[f, y, x], axis=0, keepdims=True)
    small_start(3, 1, fxe, fye)
    small_finish(3, 1, fxe, fye)
    for y in range(Y):
        fz = drv[y, XO:XO + X, :]
        energy = te[y, XO:XO + X, :]
        spread = 0.5 * (fxe[y + 2, XO + 1:XO + 1 + X, :] - fxe[y + 2, XO - 1:XO - 1 + X, :])
        spread = spread + 0.5 * (fye[y + 3, XO:XO + X, :] - fye[y + 1, XO:XO + X, :])
        spread = spread + 0.5 * (shift_up(fz) - shift_down(fz))
        put_plane(2, 0, y, energy)
        put_plane(2, 1, y, energy - flux_weight * spread)
    psum_start(2, 2)
    psum_finish(2, 2)
    unpack(2, 0, pe)
    unpack(2, 1, fye)
    for sweep in range(SWEEPS):
        small_start(4 + sweep, 1, pe, pe)
        small_finish(4 + sweep, 1, pe, pe)
        potential = []
        for y in range(Y):
            p = pe[y + 2, XO:XO + X, :]
            k = 1.0 / (1.0 + p * p)
            weighted = diffusion_mass * fye[y + 2, XO:XO + X, :]
            weights = jnp.full_like(p, diffusion_mass)
            for n in (pe[y + 2, XO - 1:XO - 1 + X, :], pe[y + 2, XO + 1:XO + 1 + X, :],
                      pe[y + 1, XO:XO + X, :], pe[y + 3, XO:XO + X, :], shift_down(p), shift_up(p)):
                couple = 0.5 * (k + 1.0 / (1.0 + n * n))
                weighted = weighted + couple * n
                weights = weights + couple
            potential.append(weighted / weights)
        for y in range(Y):
            pe[y + 2, XO:XO + X, :] = potential[y]

    for y in range(Y):
        value = pe[y + 2, XO:XO + X, :]
        temp_out[pl.ds(y, X, stride=Y), :] = value
        cb[y + 2, XO:XO + X, :] = 2.0 * h * value / (2.0 * re[y + 2, XO:XO + X, :] + h)

    @pl.loop(0, X)
    def _(x):
        for y in range(Y):
            a, b = row(ca, y + 2, XO + x), row(cb, y + 2, XO + x)
            for g in range(G):
                out[pl.ds(g * U * N + x * Y + y, U, stride=N), :] = a * q2[g, y, x] + b

    for side in range(4):
        @pl.when(has[side])
        def _():
            for ev in range(4 + SWEEPS):
                small_copy(ev, 2 if ev < 3 else 1, side).wait_send()
            for t in range(2):
                @pl.loop(0, G)
                def _(g):
                    big(t, g, side, True).wait_send()
    for ev in range(3):
        for k in range(1, NO):
            psum_scatter_copy(ev, 2 if ev == 2 else 1, k).wait_send()
            psum_gather_copy(ev, 2 if ev == 2 else 1, k, mo).wait_send()


def solution(mesh):
    NO, NX, NY = (mesh.shape[name] for name in ("ord", "gx", "gy"))

    def local(distribution, relaxation):
        O, X, Y, Z = distribution.shape
        G, U, N = O // LANE_GROUP, LANE_GROUP, X * Y
        R = N // NO
        speeds = directions(lax.axis_index("ord") * O, O)
        speeds = jnp.broadcast_to(speeds.reshape(3, G, U, 1), (3, G, U, Z))
        XA = X + 16
        v = lambda *s: pltpu.VMEM(s, f32)
        dma = lambda *s: pltpu.SemaphoreType.DMA(s)
        import functools
        scratch = [
            v(G, Y, X, U, Z), v(G, Y, X, U, Z), v(G, Y, X, U, Z), v(Y + 4, X + 4, U, Z),
            v(2, 2, G, Y, 2, U, Z), v(2, 2, G, 2, X, U, Z), v(4, Y, X, U, Z), v(N, Z),
            v(Y + 4, XA, Z), v(Y + 4, XA, Z), v(Y + 4, XA, Z), v(Y + 4, XA, Z), v(Y + 4, XA, Z), v(Y + 4, XA, Z),
            v(Y, X + 8, Z), v(Y, X + 8, Z), v(Y + 1, X, Z), v(Y + 1, X, Z), v(Y, X, Z), v(Y, X, Z), v(Y, X, Z),
            v(Y + 4, XA, Z), v(Y + 4, XA, Z),
            v(3, NO, 2, R, Z), v(3, NO, 2, R, Z), v(3, NO, 2, R, Z),
            v(4 + SWEEPS, 2, 2, Y, Z), v(4 + SWEEPS, 2, 2, X, Z), v(4 + SWEEPS, 2, 2, Y, Z), v(4 + SWEEPS, 2, 2, X, Z),
            dma(2, G, 4), dma(2, G, 4), dma(4 + SWEEPS, 4), dma(4 + SWEEPS, 4), dma(3, 2, NO), dma(3, 2, NO),
        ]
        updated, temperature = pl.pallas_call(
            functools.partial(kernel, (NO, NX, NY, O, X, Y, Z)),
            out_shape=(jax.ShapeDtypeStruct((O * N, Z), f32), jax.ShapeDtypeStruct((N, Z), f32)),
            in_specs=[pl.BlockSpec(memory_space=pltpu.VMEM)] * 3,
            out_specs=[pl.BlockSpec(memory_space=pltpu.VMEM)] * 2,
            scratch_shapes=scratch,
            compiler_params=pltpu.CompilerParams(collective_id=0, has_side_effects=True, vmem_limit_bytes=48 * 2**20),
        )(speeds, distribution.reshape(O * N, Z), relaxation.reshape(N, Z))
        return updated.reshape(O, X, Y, Z), temperature.reshape(X, Y, Z)

    return jax.shard_map(
        local,
        mesh=mesh,
        in_specs=(P("ord", "gx", "gy", None), P("gx", "gy", None)),
        out_specs=(P("ord", "gx", "gy", None), P("gx", "gy", None)),
        check_vma=False,
    )
```

```python
import jax
import jax.numpy as jnp
from jax import lax
from jax.experimental import pallas as pl
from jax.experimental.pallas import tpu as pltpu
from jax.sharding import PartitionSpec as P

NORD = 256
STEPS = 2
SWEEPS = 3
LANE_GROUP = 8

h = 0.4
eps = 0.01
diffusion_mass = 0.5
flux_weight = 2.0
golden_turn = 2.399963229728653
MESH = pl.DeviceIdType.MESH
f32 = jnp.float32


def directions(offset, length):
    ordinal = (offset + jnp.arange(length, dtype=jnp.int32)).astype(jnp.float32)
    height = 1.0 - (2.0 * ordinal + 1.0) / NORD
    radius = jnp.sqrt(1.0 - height * height)
    turned = golden_turn * ordinal
    return jnp.stack([radius * jnp.cos(turned), radius * jnp.sin(turned), height])


def slope_of(a, b, aa, bb):
    return (a + b) * (a * b + eps) / (aa + bb)


def kernel(dims, speed, dist, relax, out, temp_out, *scratch):
    NO, NX, NY, O, X, Y, Z = dims
    (q0, q1, q2, src, hx, hy, acc, tmix, te, re, pe, fxe, fye, drv, px, qx, py, qy, pz, dqz,
     ca, cb, part, rbuf, full, ssx, ssy, hsx, hsy, b_send, b_recv, s_send, s_recv, p_send, p_recv) = scratch
    G = O // LANE_GROUP
    N = X * Y
    R = N // NO
    U = LANE_GROUP
    XO = 8
    mo, mx, my = lax.axis_index("ord"), lax.axis_index("gx"), lax.axis_index("gy")
    has = (mx > 0, mx < NX - 1, my > 0, my < NY - 1)
    peer = ({"gx": mx - 1}, {"gx": mx + 1}, {"gy": my - 1}, {"gy": my + 1})

    barrier = pltpu.get_barrier_semaphore()
    for k in range(1, NO):
        pl.semaphore_signal(barrier, inc=1, device_id={"ord": lax.rem(mo + k, NO)}, device_id_type=MESH)
    for side in range(4):
        @pl.when(has[side])
        def _():
            pl.semaphore_signal(barrier, inc=1, device_id=peer[side], device_id_type=MESH)
    ends = sum((jnp.where(flag, 1, 0) for flag in has), 0)
    pl.semaphore_wait(barrier, NO - 1 + ends)

    def small_copy(ev, layers, side):
        buf_s, buf_r = (ssx, hsx) if side < 2 else (ssy, hsy)
        mine, theirs = side % 2, 1 - side % 2
        return pltpu.make_async_remote_copy(
            src_ref=buf_s.at[ev, mine, pl.ds(0, layers)],
            dst_ref=buf_r.at[ev, theirs, pl.ds(0, layers)],
            send_sem=s_send.at[ev, side],
            recv_sem=s_recv.at[ev, side ^ 1],
            device_id=peer[side], device_id_type=MESH)

    def small_recv(ev, layers, side):
        buf_s, buf_r = (ssx, hsx) if side < 2 else (ssy, hsy)
        return pltpu.make_async_remote_copy(
            src_ref=buf_s.at[ev, side % 2, pl.ds(0, layers)],
            dst_ref=buf_r.at[ev, side % 2, pl.ds(0, layers)],
            send_sem=s_send.at[ev, side],
            recv_sem=s_recv.at[ev, side],
            device_id=peer[side], device_id_type=MESH)

    def small_start(ev, layers, fx, fy):
        for l in range(layers):
            for y in range(Y):
                ssx[ev, 0, l, y:y + 1, :] = fx[y + 2, XO + l:XO + l + 1, :]
                ssx[ev, 1, l, y:y + 1, :] = fx[y + 2, XO + X - layers + l:XO + X - layers + l + 1, :]
            ssy[ev, 0, l] = fy[2 + l, XO:XO + X, :]
            ssy[ev, 1, l] = fy[2 + Y - layers + l, XO:XO + X, :]
        for side in range(4):
            @pl.when(has[side])
            def _():
                small_copy(ev, layers, side).start()

    def small_finish(ev, layers, fx, fy):
        for side in range(4):
            @pl.when(has[side])
            def _():
                small_recv(ev, layers, side).wait_recv()
                for l in range(layers):
                    if side < 2:
                        at = XO - layers + l if side == 0 else XO + X + l
                        for y in range(Y):
                            fx[y + 2, at:at + 1, :] = hsx[ev, side % 2, l, y:y + 1, :]
                    else:
                        at = 2 - layers + l if side == 2 else 2 + Y + l
                        fy[at, XO:XO + X, :] = hsy[ev, side % 2, l]

    bigs = (q0, q1)

    def big(t, g, side, sending):
        q = bigs[t]
        if side < 2:
            lo = 0 if side == 0 else X - 2
            s = q.at[g, :, pl.ds(lo, 2)]
            buf = hx
        else:
            lo = 0 if side == 2 else Y - 2
            s = q.at[g, pl.ds(lo, 2)]
            buf = hy
        slot = (1 - side % 2) if sending else side % 2
        return pltpu.make_async_remote_copy(
            src_ref=s, dst_ref=buf.at[t, slot, g],
            send_sem=b_send.at[t, g, side],
            recv_sem=b_recv.at[t, g, side ^ 1 if sending else side],
            device_id=peer[side], device_id_type=MESH)

    def psum_scatter_copy(ev, fields, k):
        to = lax.rem(mo + k, NO)
        return pltpu.make_async_remote_copy(
            src_ref=part.at[ev, to, pl.ds(0, fields)], dst_ref=rbuf.at[ev, k, pl.ds(0, fields)],
            send_sem=p_send.at[ev, 0, k], recv_sem=p_recv.at[ev, 0, k],
            device_id={"ord": to}, device_id_type=MESH)

    def psum_gather_copy(ev, fields, k, owner):
        to = lax.rem(mo + k, NO)
        return pltpu.make_async_remote_copy(
            src_ref=full.at[ev, mo, pl.ds(0, fields)], dst_ref=full.at[ev, owner, pl.ds(0, fields)],
            send_sem=p_send.at[ev, 1, k], recv_sem=p_recv.at[ev, 1, k],
            device_id={"ord": to}, device_id_type=MESH)

    def psum_start(ev, fields):
        for k in range(1, NO):
            psum_scatter_copy(ev, fields, k).start()

    def psum_finish(ev, fields):
        for k in range(1, NO):
            psum_scatter_copy(ev, fields, k).wait_recv()
        for f in range(fields):
            total = part[ev, mo, f]
            for k in range(1, NO):
                total = total + rbuf[ev, k, f]
            full[ev, mo, f] = total * (1.0 / NORD)
        for k in range(1, NO):
            psum_gather_copy(ev, fields, k, mo).start()
        for k in range(1, NO):
            psum_gather_copy(ev, fields, k, lax.rem(mo + NO - k, NO)).wait_recv()

    def rows(r):
        return r // R, r % R

    def unpack(ev, f, dst):
        for y in range(Y):
            for n in range(max(1, X // R)):
                size = min(R, X)
                r0 = y * X + n * size
                dst[y + 2, XO + n * size:XO + (n + 1) * size, :] = full[ev, r0 // R, f, r0 % R:r0 % R + size, :]

    def put_plane(ev, f, y, value):
        size = min(R, X)
        for n in range(X // size):
            r0 = y * X + n * size
            part[ev, r0 // R, f, r0 % R:r0 % R + size, :] = value[n * size:(n + 1) * size]

    for ref in (te, re, pe, fxe, fye):
        ref[...] = jnp.zeros_like(ref)
    for y in range(Y):
        re[y + 2, XO:XO + X, :] = relax[pl.ds(y, X, stride=Y), :]
    small_start(0, 2, re, re)

    @pl.loop(0, N // 8)
    def _(i):
        at = pl.multiple_of(i * 8, 8)
        total = dist[0, pl.ds(at, 8), :]
        for o in range(1, O):
            total = total + dist[o, pl.ds(at, 8), :]
        tmix[pl.ds(at, 8), :] = total
    for y in range(Y):
        put_plane(0, 0, y, tmix[pl.ds(y, X, stride=Y), :])
    psum_start(0, 1)

    def place(i, j):
        if U % Y == 0:
            return j % Y, i * (U // Y) + j // Y
        return lax.rem(i * U + j, Y), (i * U + j) // Y

    def big_start(t, g):
        for side in range(4):
            @pl.when(has[side])
            def _():
                big(t, g, side, True).start()

    def transpose_in(g):
        @pl.loop(0, N // U)
        def _(i):
            block = jnp.swapaxes(dist[pl.ds(g * U, U), pl.ds(pl.multiple_of(i * U, U), U), :], 0, 1)
            for j in range(U):
                y, x = place(i, j)
                q0[g, y, x] = block[j]

    transpose_in(0)
    big_start(0, 0)

    @pl.loop(1, G)
    def _(g):
        transpose_in(g)

    src[...] = jnp.zeros_like(src)
    small_finish(0, 2, re, re)
    lane = lax.broadcasted_iota(jnp.int32, (X, Z), 1)

    def shift_up(v):
        return jnp.where(lane == Z - 1, 0.0, pltpu.roll(v, Z - 1, 1))

    def shift_down(v):
        return jnp.where(lane == 0, 0.0, pltpu.roll(v, 1, 1))

    XA = X + 2 * XO

    def face_r(r0, r1):
        r = 0.5 * (r0 + r1)
        return 2.0 * r / (2.0 * r + 0.5 * h)

    def face_t(t0, t1, p):
        return 0.5 * (t0 + t1) * (1.0 - p)

    for y in range(Y + 4):
        r = re[y]
        ca[y] = (2.0 * r - h) / (2.0 * r + h)
    for y in range(Y):
        r = re[y + 2, XO:XO + X, :]
        px[y, 0:X, :] = face_r(re[y + 2, XO - 1:XO - 1 + X, :], r)
        px[y, X:X + 1, :] = face_r(re[y + 2, XO + X - 1:XO + X, :], re[y + 2, XO + X:XO + X + 1, :])
        pz[0, y] = face_r(r, shift_up(r))
        pz[1, y] = face_r(shift_down(r), r)
    for y in range(Y + 1):
        py[y] = face_r(re[y + 1, XO:XO + X, :], re[y + 2, XO:XO + X, :])

    def coefficients():
        for y in range(Y + 4):
            cb[y] = 2.0 * h * te[y] / (2.0 * re[y] + h)
        for y in range(Y):
            t = te[y + 2, XO:XO + X, :]
            qx[y, 0:X, :] = face_t(te[y + 2, XO - 1:XO - 1 + X, :], t, px[y, 0:X, :])
            qx[y, X:X + 1, :] = face_t(te[y + 2, XO + X - 1:XO + X, :], te[y + 2, XO + X:XO + X + 1, :], px[y, X:X + 1, :])
            inflow = face_t(t, shift_up(t), pz[0, y]) - face_t(shift_down(t), t, pz[1, y])
            dqz[0, y] = inflow
            dqz[1, y] = -inflow
        for y in range(Y + 1):
            qy[y] = face_t(te[y + 1, XO:XO + X, :], te[y + 2, XO:XO + X, :], py[y])

    def row(ref, y, x):
        return jnp.broadcast_to(ref[y, pl.ds(x, 1), :], (U, Z))

    lane8 = lax.broadcasted_iota(jnp.int32, (U, Z), 1)

    def advance(t, g):
        q, qn = (q0, q1, q2)[t], (q0, q1, q2)[t + 1]

        @pl.loop(0, X, unroll=2)
        def _(x):
            for y in range(Y):
                src[y + 2, x + 2] = row(ca, y + 2, XO + x) * q[g, y, x] + row(cb, y + 2, XO + x)
        for side in range(4):
            @pl.when(has[side])
            def _():
                big(t, g, side, False).wait_recv()
                if side < 2:
                    for l in range(2):
                        x = (l - 2) if side == 0 else X + l
                        for y in range(Y):
                            src[y + 2, x + 2] = row(ca, y + 2, XO + x) * hx[t, side, g, y, l] + row(cb, y + 2, XO + x)
                else:
                    @pl.loop(0, X, unroll=4)
                    def _(x):
                        for l in range(2):
                            y = (l - 2) if side == 2 else Y + l
                            src[y + 2, x + 2] = row(ca, y + 2, XO + x) * hy[t, side - 2, g, l, x] + row(cb, y + 2, XO + x)

        cx, cy, cz = speed[0, g], speed[1, g], speed[2, g]

        def gamma(c):
            return jnp.where(c >= 0.0, 0.5 * (1.0 - h * c), -0.5 * (1.0 + h * c))

        gx_, gy_, gz_ = gamma(cx), gamma(cy), gamma(cz)
        gz_eps = jnp.abs(gz_) * eps
        hcx, hcy, hcz = h * cx, h * cy, h * jnp.abs(cz)
        upward = mo * O + g * U < NORD // 2
        shift = jnp.where(upward, 1, Z - 1)
        own = jnp.where(upward, 0, 1)
        inlet = lane8 == jnp.where(upward, 0, Z - 1)

        start = []
        for y in range(Y):
            sm2, sm1, s0, s1 = (src[y + 2, i] for i in range(4))
            a, b, c = sm1 - sm2, s0 - sm1, s1 - s0
            aa, bb, cc = a * a + eps, b * b + eps, c * c + eps
            um = sm1 + gx_ * slope_of(a, b, aa, bb)
            u0 = s0 + gx_ * slope_of(b, c, bb, cc)
            e0 = row(px, y, 0) * jnp.where(cx >= 0.0, um, u0) + row(qx, y, 0)
            start += [u0, e0, c]

        def body(x, carry):
            posx, posy = cx >= 0.0, cy >= 0.0
            column = [src[j, x + 2] for j in range(Y + 4)]
            d = [column[j + 1] - column[j] for j in range(Y + 3)]
            e = [None] + [d[j] * d[j] + eps for j in range(1, Y + 2)]
            u = [None, None] + [column[j] + gy_ * slope_of(d[j - 1], d[j], e[j - 1], e[j]) for j in range(2, Y + 2)] + [None]
            oa, ob = jnp.where(posy, d[0], d[Y + 1]), jnp.where(posy, d[1], d[Y + 2])
            beyond = jnp.where(posy, column[1], column[Y + 2]) + gy_ * slope_of(oa, ob, oa * oa + eps, ob * ob + eps)
            u[1] = u[Y + 2] = beyond
            ey = [row(py, f, x) * jnp.where(posy, u[f + 1], u[f + 2]) + row(qy, f, x) for f in range(Y + 1)]
            carried = []
            for y in range(Y):
                s = column[y + 2]
                u0, e0, c = carry[3 * y:3 * y + 3]
                s1, s2 = src[y + 2, x + 3], src[y + 2, x + 4]
                d1 = s2 - s1
                u1 = s1 + gx_ * slope_of(c, d1, c * c + eps, d1 * d1 + eps)
                e1 = row(px, y, x + 1) * jnp.where(posx, u0, u1) + row(qx, y, x + 1)
                carried += [u1, e1, d1]
                zb = jnp.where(lane8 == Z - 1, 0.0, pltpu.roll(s, Z - 1, 1)) - s
                za = jnp.where(lane8 == 0, s, pltpu.roll(zb, 1, 1))
                uz = s + gz_ * slope_of(za, zb, za * za + eps, zb * zb + eps)
                ghost = gz_eps * s / (s * s + 2.0 * eps)
                wz = jnp.where(inlet, ghost, pltpu.roll(uz, shift, 1))
                fz = row(pz.at[own], y, x) * uz - row(pz.at[1 - own], y, x) * wz + row(dqz.at[own], y, x)
                new = s - (hcx * (e1 - e0) + hcy * (ey[y + 1] - ey[y]) + hcz * fz)
                qn[g, y, x] = new
                if t == 0:
                    acc[0, y, x] += new
                else:
                    acc[0, y, x] += new
                    acc[1, y, x] += cx * new
                    acc[2, y, x] += cy * new
                    acc[3, y, x] += cz * new
            return tuple(carried)

        lax.fori_loop(0, X, body, tuple(start), unroll=2)

    def fold(fields):
        @pl.loop(0, X // U)
        def _(i):
            at = pl.multiple_of(i * U, U)
            for f, (dst, first) in enumerate(fields):
                for y in range(Y):
                    total = jnp.sum(jnp.swapaxes(acc[f, y, pl.ds(at, U)], 0, 1), axis=0)
                    dst[first + y, pl.ds(pl.multiple_of(XO + at, U), U), :] = total

    for t in range(STEPS):
        psum_finish(t, 1)
        unpack(t, 0, te)
        small_start(1 + t, 2, te, te)
        if t == 0:
            @pl.loop(1, G)
            def _(g):
                big_start(0, g)
        for f in range(4 if t else 1):
            acc[f] = jnp.zeros_like(acc[f])
        small_finish(1 + t, 2, te, te)
        coefficients()

        @pl.loop(0, G)
        def _(g):
            advance(t, g)
            if t + 1 < STEPS:
                big_start(t + 1, g)

        if t + 1 < STEPS:
            fold([(drv, 0)])
            for y in range(Y):
                put_plane(t + 1, 0, y, drv[y, XO:XO + X, :])
            psum_start(t + 1, 1)

    fold([(te, 0), (fxe, 2), (fye, 2), (drv, 0)])
    small_start(3, 1, fxe, fye)
    small_finish(3, 1, fxe, fye)
    for y in range(Y):
        fz = drv[y, XO:XO + X, :]
        energy = te[y, XO:XO + X, :]
        spread = 0.5 * (fxe[y + 2, XO + 1:XO + 1 + X, :] - fxe[y + 2, XO - 1:XO - 1 + X, :])
        spread = spread + 0.5 * (fye[y + 3, XO:XO + X, :] - fye[y + 1, XO:XO + X, :])
        spread = spread + 0.5 * (shift_up(fz) - shift_down(fz))
        put_plane(2, 0, y, energy)
        put_plane(2, 1, y, energy - flux_weight * spread)
    psum_start(2, 2)
    psum_finish(2, 2)
    unpack(2, 0, pe)
    unpack(2, 1, fye)
    for sweep in range(SWEEPS):
        small_start(4 + sweep, 1, pe, pe)
        small_finish(4 + sweep, 1, pe, pe)
        potential = []
        for y in range(Y):
            p = pe[y + 2, XO:XO + X, :]
            k = 1.0 / (1.0 + p * p)
            weighted = diffusion_mass * fye[y + 2, XO:XO + X, :]
            weights = jnp.full_like(p, diffusion_mass)
            for n in (pe[y + 2, XO - 1:XO - 1 + X, :], pe[y + 2, XO + 1:XO + 1 + X, :],
                      pe[y + 1, XO:XO + X, :], pe[y + 3, XO:XO + X, :], shift_down(p), shift_up(p)):
                couple = 0.5 * (k + 1.0 / (1.0 + n * n))
                weighted = weighted + couple * n
                weights = weights + couple
            potential.append(weighted / weights)
        for y in range(Y):
            pe[y + 2, XO:XO + X, :] = potential[y]

    for y in range(Y):
        value = pe[y + 2, XO:XO + X, :]
        temp_out[pl.ds(y, X, stride=Y), :] = value
        cb[y + 2, XO:XO + X, :] = 2.0 * h * value / (2.0 * re[y + 2, XO:XO + X, :] + h)

    @pl.loop(0, N // U)
    def _(i):
        at = [place(i, j) for j in range(U)]
        a = [row(ca, y + 2, XO + x) for y, x in at]
        b = [row(cb, y + 2, XO + x) for y, x in at]
        for g in range(G):
            block = jnp.stack([a[j] * q2[g, at[j][0], at[j][1]] + b[j] for j in range(U)])
            out[pl.ds(g * U, U), pl.ds(pl.multiple_of(i * U, U), U), :] = jnp.swapaxes(block, 0, 1)

    for side in range(4):
        @pl.when(has[side])
        def _():
            for ev in range(4 + SWEEPS):
                small_copy(ev, 2 if ev < 3 else 1, side).wait_send()
            for t in range(2):
                @pl.loop(0, G)
                def _(g):
                    big(t, g, side, True).wait_send()
    for ev in range(3):
        for k in range(1, NO):
            psum_scatter_copy(ev, 2 if ev == 2 else 1, k).wait_send()
            psum_gather_copy(ev, 2 if ev == 2 else 1, k, mo).wait_send()


def solution(mesh):
    NO, NX, NY = (mesh.shape[name] for name in ("ord", "gx", "gy"))

    def local(distribution, relaxation):
        O, X, Y, Z = distribution.shape
        G, U, N = O // LANE_GROUP, LANE_GROUP, X * Y
        R = N // NO
        speeds = directions(lax.axis_index("ord") * O, O)
        speeds = jnp.broadcast_to(speeds.reshape(3, G, U, 1), (3, G, U, Z))
        XA = X + 16
        v = lambda *s: pltpu.VMEM(s, f32)
        dma = lambda *s: pltpu.SemaphoreType.DMA(s)
        import functools
        scratch = [
            v(G, Y, X, U, Z), v(G, Y, X, U, Z), v(G, Y, X, U, Z), v(Y + 4, X + 4, U, Z),
            v(2, 2, G, Y, 2, U, Z), v(2, 2, G, 2, X, U, Z), v(4, Y, X, U, Z), v(N, Z),
            v(Y + 4, XA, Z), v(Y + 4, XA, Z), v(Y + 4, XA, Z), v(Y + 4, XA, Z), v(Y + 4, XA, Z), v(Y + 4, XA, Z),
            v(Y, X + 8, Z), v(Y, X + 8, Z), v(Y + 1, X, Z), v(Y + 1, X, Z), v(2, Y, X, Z), v(2, Y, X, Z),
            v(Y + 4, XA, Z), v(Y + 4, XA, Z),
            v(3, NO, 2, R, Z), v(3, NO, 2, R, Z), v(3, NO, 2, R, Z),
            v(4 + SWEEPS, 2, 2, Y, Z), v(4 + SWEEPS, 2, 2, X, Z), v(4 + SWEEPS, 2, 2, Y, Z), v(4 + SWEEPS, 2, 2, X, Z),
            dma(2, G, 4), dma(2, G, 4), dma(4 + SWEEPS, 4), dma(4 + SWEEPS, 4), dma(3, 2, NO), dma(3, 2, NO),
        ]
        updated, temperature = pl.pallas_call(
            functools.partial(kernel, (NO, NX, NY, O, X, Y, Z)),
            out_shape=(jax.ShapeDtypeStruct((O, N, Z), f32), jax.ShapeDtypeStruct((N, Z), f32)),
            in_specs=[pl.BlockSpec(memory_space=pltpu.VMEM)] * 3,
            out_specs=[pl.BlockSpec(memory_space=pltpu.VMEM)] * 2,
            scratch_shapes=scratch,
            compiler_params=pltpu.CompilerParams(collective_id=0, has_side_effects=True, vmem_limit_bytes=48 * 2**20),
        )(speeds, distribution.reshape(O, N, Z), relaxation.reshape(N, Z))
        return updated.reshape(O, X, Y, Z), temperature.reshape(X, Y, Z)

    return jax.shard_map(
        local,
        mesh=mesh,
        in_specs=(P("ord", "gx", "gy", None), P("gx", "gy", None)),
        out_specs=(P("ord", "gx", "gy", None), P("gx", "gy", None)),
        check_vma=False,
    )
```

```python
import jax
import jax.numpy as jnp
from jax import lax
from jax.experimental import pallas as pl
from jax.experimental.pallas import tpu as pltpu
from jax.sharding import PartitionSpec as P

NORD = 256
STEPS = 2
SWEEPS = 3
LANE_GROUP = 8

h = 0.4
eps = 0.01
diffusion_mass = 0.5
flux_weight = 2.0
golden_turn = 2.399963229728653
MESH = pl.DeviceIdType.MESH
f32 = jnp.float32


def directions(offset, length):
    ordinal = (offset + jnp.arange(length, dtype=jnp.int32)).astype(jnp.float32)
    height = 1.0 - (2.0 * ordinal + 1.0) / NORD
    radius = jnp.sqrt(1.0 - height * height)
    turned = golden_turn * ordinal
    return jnp.stack([radius * jnp.cos(turned), radius * jnp.sin(turned), height])


def slope_of(a, b, aa, bb):
    return (a + b) * (a * b + eps) / (aa + bb)


def kernel(dims, speed, dist, relax, out, temp_out, *scratch):
    NO, NX, NY, O, X, Y, Z = dims
    (q0, q1, q2, src, hx, hy, acc, tmix, te, re, pe, fxe, fye, drv, px, qx, py, qy, pz, dqz,
     ca, cb, part, rbuf, full, ssx, ssy, hsx, hsy, b_send, b_recv, s_send, s_recv, p_send, p_recv) = scratch
    G = O // LANE_GROUP
    N = X * Y
    R = N // NO
    U = LANE_GROUP
    XO = 8
    EARLY = (1, (G + 1) // 2)
    mo, mx, my = lax.axis_index("ord"), lax.axis_index("gx"), lax.axis_index("gy")
    has = (mx > 0, mx < NX - 1, my > 0, my < NY - 1)
    peer = ({"gx": mx - 1}, {"gx": mx + 1}, {"gy": my - 1}, {"gy": my + 1})

    barrier = pltpu.get_barrier_semaphore()
    for k in range(1, NO):
        pl.semaphore_signal(barrier, inc=1, device_id={"ord": lax.rem(mo + k, NO)}, device_id_type=MESH)
    for side in range(4):
        @pl.when(has[side])
        def _():
            pl.semaphore_signal(barrier, inc=1, device_id=peer[side], device_id_type=MESH)
    ends = sum((jnp.where(flag, 1, 0) for flag in has), 0)
    pl.semaphore_wait(barrier, NO - 1 + ends)

    def small_copy(ev, layers, side):
        buf_s, buf_r = (ssx, hsx) if side < 2 else (ssy, hsy)
        mine, theirs = side % 2, 1 - side % 2
        return pltpu.make_async_remote_copy(
            src_ref=buf_s.at[ev, mine, pl.ds(0, layers)],
            dst_ref=buf_r.at[ev, theirs, pl.ds(0, layers)],
            send_sem=s_send.at[ev, side],
            recv_sem=s_recv.at[ev, side ^ 1],
            device_id=peer[side], device_id_type=MESH)

    def small_recv(ev, layers, side):
        buf_s, buf_r = (ssx, hsx) if side < 2 else (ssy, hsy)
        return pltpu.make_async_remote_copy(
            src_ref=buf_s.at[ev, side % 2, pl.ds(0, layers)],
            dst_ref=buf_r.at[ev, side % 2, pl.ds(0, layers)],
            send_sem=s_send.at[ev, side],
            recv_sem=s_recv.at[ev, side],
            device_id=peer[side], device_id_type=MESH)

    def small_start(ev, layers, fx, fy):
        for l in range(layers):
            for y in range(Y):
                ssx[ev, 0, l, y:y + 1, :] = fx[y + 2, XO + l:XO + l + 1, :]
                ssx[ev, 1, l, y:y + 1, :] = fx[y + 2, XO + X - layers + l:XO + X - layers + l + 1, :]
            ssy[ev, 0, l] = fy[2 + l, XO:XO + X, :]
            ssy[ev, 1, l] = fy[2 + Y - layers + l, XO:XO + X, :]
        for side in range(4):
            @pl.when(has[side])
            def _():
                small_copy(ev, layers, side).start()

    def small_finish(ev, layers, fx, fy):
        for side in range(4):
            @pl.when(has[side])
            def _():
                small_recv(ev, layers, side).wait_recv()
                for l in range(layers):
                    if side < 2:
                        at = XO - layers + l if side == 0 else XO + X + l
                        for y in range(Y):
                            fx[y + 2, at:at + 1, :] = hsx[ev, side % 2, l, y:y + 1, :]
                    else:
                        at = 2 - layers + l if side == 2 else 2 + Y + l
                        fy[at, XO:XO + X, :] = hsy[ev, side % 2, l]

    bigs = (q0, q1)

    def big(t, g, side, sending):
        q = bigs[t]
        if side < 2:
            lo = 0 if side == 0 else X - 2
            s = q.at[g, :, pl.ds(lo, 2)]
            buf = hx
        else:
            lo = 0 if side == 2 else Y - 2
            s = q.at[g, pl.ds(lo, 2)]
            buf = hy
        slot = (1 - side % 2) if sending else side % 2
        return pltpu.make_async_remote_copy(
            src_ref=s, dst_ref=buf.at[t, slot, g],
            send_sem=b_send.at[t, g, side],
            recv_sem=b_recv.at[t, g, side ^ 1 if sending else side],
            device_id=peer[side], device_id_type=MESH)

    def psum_scatter_copy(ev, fields, k):
        to = lax.rem(mo + k, NO)
        return pltpu.make_async_remote_copy(
            src_ref=part.at[ev, to, pl.ds(0, fields)], dst_ref=rbuf.at[ev, k, pl.ds(0, fields)],
            send_sem=p_send.at[ev, 0, k], recv_sem=p_recv.at[ev, 0, k],
            device_id={"ord": to}, device_id_type=MESH)

    def psum_gather_copy(ev, fields, k, owner):
        to = lax.rem(mo + k, NO)
        return pltpu.make_async_remote_copy(
            src_ref=full.at[ev, mo, pl.ds(0, fields)], dst_ref=full.at[ev, owner, pl.ds(0, fields)],
            send_sem=p_send.at[ev, 1, k], recv_sem=p_recv.at[ev, 1, k],
            device_id={"ord": to}, device_id_type=MESH)

    def psum_start(ev, fields):
        for k in range(1, NO):
            psum_scatter_copy(ev, fields, k).start()

    def psum_finish(ev, fields):
        for k in range(1, NO):
            psum_scatter_copy(ev, fields, k).wait_recv()
        for f in range(fields):
            total = part[ev, mo, f]
            for k in range(1, NO):
                total = total + rbuf[ev, k, f]
            full[ev, mo, f] = total * (1.0 / NORD)
        for k in range(1, NO):
            psum_gather_copy(ev, fields, k, mo).start()
        for k in range(1, NO):
            psum_gather_copy(ev, fields, k, lax.rem(mo + NO - k, NO)).wait_recv()

    def rows(r):
        return r // R, r % R

    def unpack(ev, f, dst):
        for y in range(Y):
            for n in range(max(1, X // R)):
                size = min(R, X)
                r0 = y * X + n * size
                dst[y + 2, XO + n * size:XO + (n + 1) * size, :] = full[ev, r0 // R, f, r0 % R:r0 % R + size, :]

    def put_plane(ev, f, y, value):
        size = min(R, X)
        for n in range(X // size):
            r0 = y * X + n * size
            part[ev, r0 // R, f, r0 % R:r0 % R + size, :] = value[n * size:(n + 1) * size]

    for ref in (te, re, pe, fxe, fye):
        ref[...] = jnp.zeros_like(ref)
    for y in range(Y):
        re[y + 2, XO:XO + X, :] = relax[pl.ds(y, X, stride=Y), :]
    small_start(0, 2, re, re)

    @pl.loop(0, N // 8)
    def _(i):
        at = pl.multiple_of(i * 8, 8)
        total = dist[0, pl.ds(at, 8), :]
        for o in range(1, O):
            total = total + dist[o, pl.ds(at, 8), :]
        tmix[pl.ds(at, 8), :] = total
    for y in range(Y):
        put_plane(0, 0, y, tmix[pl.ds(y, X, stride=Y), :])
    psum_start(0, 1)

    def place(i, j):
        if U % Y == 0:
            return j % Y, i * (U // Y) + j // Y
        return lax.rem(i * U + j, Y), (i * U + j) // Y

    def big_start(t, g):
        for side in range(4):
            @pl.when(has[side])
            def _():
                big(t, g, side, True).start()

    def transpose_in(g):
        @pl.loop(0, N // U)
        def _(i):
            block = jnp.swapaxes(dist[pl.ds(g * U, U), pl.ds(pl.multiple_of(i * U, U), U), :], 0, 1)
            for j in range(U):
                y, x = place(i, j)
                q0[g, y, x] = block[j]

    transpose_in(0)
    big_start(0, 0)

    @pl.loop(1, G)
    def _(g):
        transpose_in(g)

    src[...] = jnp.zeros_like(src)
    small_finish(0, 2, re, re)
    lane = lax.broadcasted_iota(jnp.int32, (X, Z), 1)

    def shift_up(v):
        return jnp.where(lane == Z - 1, 0.0, pltpu.roll(v, Z - 1, 1))

    def shift_down(v):
        return jnp.where(lane == 0, 0.0, pltpu.roll(v, 1, 1))

    XA = X + 2 * XO

    def face_r(r0, r1):
        r = 0.5 * (r0 + r1)
        return 2.0 * r / (2.0 * r + 0.5 * h)

    def face_t(t0, t1, p):
        return 0.5 * (t0 + t1) * (1.0 - p)

    for y in range(Y + 4):
        r = re[y]
        ca[y] = (2.0 * r - h) / (2.0 * r + h)
    for y in range(Y):
        r = re[y + 2, XO:XO + X, :]
        px[y, 0:X, :] = face_r(re[y + 2, XO - 1:XO - 1 + X, :], r)
        px[y, X:X + 1, :] = face_r(re[y + 2, XO + X - 1:XO + X, :], re[y + 2, XO + X:XO + X + 1, :])
        pz[0, y] = face_r(r, shift_up(r))
        pz[1, y] = face_r(shift_down(r), r)
    for y in range(Y + 1):
        py[y] = face_r(re[y + 1, XO:XO + X, :], re[y + 2, XO:XO + X, :])

    def coefficients():
        for y in range(Y + 4):
            cb[y] = 2.0 * h * te[y] / (2.0 * re[y] + h)
        for y in range(Y):
            t = te[y + 2, XO:XO + X, :]
            qx[y, 0:X, :] = face_t(te[y + 2, XO - 1:XO - 1 + X, :], t, px[y, 0:X, :])
            qx[y, X:X + 1, :] = face_t(te[y + 2, XO + X - 1:XO + X, :], te[y + 2, XO + X:XO + X + 1, :], px[y, X:X + 1, :])
            inflow = face_t(t, shift_up(t), pz[0, y]) - face_t(shift_down(t), t, pz[1, y])
            dqz[0, y] = inflow
            dqz[1, y] = -inflow
        for y in range(Y + 1):
            qy[y] = face_t(te[y + 1, XO:XO + X, :], te[y + 2, XO:XO + X, :], py[y])

    def row(ref, y, x):
        return jnp.broadcast_to(ref[y, pl.ds(x, 1), :], (U, Z))

    lane8 = lax.broadcasted_iota(jnp.int32, (U, Z), 1)

    def advance(t, g):
        q, qn = (q0, q1, q2)[t], (q0, q1, q2)[t + 1]

        @pl.loop(0, X, unroll=2)
        def _(x):
            for y in range(Y):
                src[y + 2, x + 2] = row(ca, y + 2, XO + x) * q[g, y, x] + row(cb, y + 2, XO + x)
        for side in range(4):
            @pl.when(has[side])
            def _():
                big(t, g, side, False).wait_recv()
                if side < 2:
                    for l in range(2):
                        x = (l - 2) if side == 0 else X + l
                        for y in range(Y):
                            src[y + 2, x + 2] = row(ca, y + 2, XO + x) * hx[t, side, g, y, l] + row(cb, y + 2, XO + x)
                else:
                    @pl.loop(0, X, unroll=4)
                    def _(x):
                        for l in range(2):
                            y = (l - 2) if side == 2 else Y + l
                            src[y + 2, x + 2] = row(ca, y + 2, XO + x) * hy[t, side - 2, g, l, x] + row(cb, y + 2, XO + x)

        cx, cy, cz = speed[0, g], speed[1, g], speed[2, g]

        def gamma(c):
            return jnp.where(c >= 0.0, 0.5 * (1.0 - h * c), -0.5 * (1.0 + h * c))

        gx_, gy_, gz_ = gamma(cx), gamma(cy), gamma(cz)
        gz_eps = jnp.abs(gz_) * eps
        hcx, hcy, hcz = h * cx, h * cy, h * jnp.abs(cz)
        upward = mo * O + g * U < NORD // 2
        shift = jnp.where(upward, 1, Z - 1)
        own = jnp.where(upward, 0, 1)
        inlet = lane8 == jnp.where(upward, 0, Z - 1)

        start = []
        for y in range(Y):
            sm2, sm1, s0, s1 = (src[y + 2, i] for i in range(4))
            a, b, c = sm1 - sm2, s0 - sm1, s1 - s0
            aa, bb, cc = a * a + eps, b * b + eps, c * c + eps
            um = sm1 + gx_ * slope_of(a, b, aa, bb)
            u0 = s0 + gx_ * slope_of(b, c, bb, cc)
            e0 = row(px, y, 0) * jnp.where(cx >= 0.0, um, u0) + row(qx, y, 0)
            start += [u0, e0, c]

        def body(x, carry):
            posx, posy = cx >= 0.0, cy >= 0.0
            column = [src[j, x + 2] for j in range(Y + 4)]
            d = [column[j + 1] - column[j] for j in range(Y + 3)]
            e = [None] + [d[j] * d[j] + eps for j in range(1, Y + 2)]
            u = [None, None] + [column[j] + gy_ * slope_of(d[j - 1], d[j], e[j - 1], e[j]) for j in range(2, Y + 2)] + [None]
            oa, ob = jnp.where(posy, d[0], d[Y + 1]), jnp.where(posy, d[1], d[Y + 2])
            beyond = jnp.where(posy, column[1], column[Y + 2]) + gy_ * slope_of(oa, ob, oa * oa + eps, ob * ob + eps)
            u[1] = u[Y + 2] = beyond
            ey = [row(py, f, x) * jnp.where(posy, u[f + 1], u[f + 2]) + row(qy, f, x) for f in range(Y + 1)]
            carried = []
            for y in range(Y):
                s = column[y + 2]
                u0, e0, c = carry[3 * y:3 * y + 3]
                s1, s2 = src[y + 2, x + 3], src[y + 2, x + 4]
                d1 = s2 - s1
                u1 = s1 + gx_ * slope_of(c, d1, c * c + eps, d1 * d1 + eps)
                e1 = row(px, y, x + 1) * jnp.where(posx, u0, u1) + row(qx, y, x + 1)
                carried += [u1, e1, d1]
                zb = jnp.where(lane8 == Z - 1, 0.0, pltpu.roll(s, Z - 1, 1)) - s
                za = jnp.where(lane8 == 0, s, pltpu.roll(zb, 1, 1))
                uz = s + gz_ * slope_of(za, zb, za * za + eps, zb * zb + eps)
                ghost = gz_eps * s / (s * s + 2.0 * eps)
                wz = jnp.where(inlet, ghost, pltpu.roll(uz, shift, 1))
                fz = row(pz.at[own], y, x) * uz - row(pz.at[1 - own], y, x) * wz + row(dqz.at[own], y, x)
                new = s - (hcx * (e1 - e0) + hcy * (ey[y + 1] - ey[y]) + hcz * fz)
                qn[g, y, x] = new
                if t == 0:
                    acc[0, y, x] += new
                else:
                    acc[0, y, x] += new
                    acc[1, y, x] += cx * new
                    acc[2, y, x] += cy * new
                    acc[3, y, x] += cz * new
            return tuple(carried)

        lax.fori_loop(0, X, body, tuple(start), unroll=2)

    def fold(fields):
        @pl.loop(0, X // U)
        def _(i):
            at = pl.multiple_of(i * U, U)
            for f, (dst, first) in enumerate(fields):
                for y in range(Y):
                    total = jnp.sum(jnp.swapaxes(acc[f, y, pl.ds(at, U)], 0, 1), axis=0)
                    dst[first + y, pl.ds(pl.multiple_of(XO + at, U), U), :] = total

    for t in range(STEPS):
        psum_finish(t, 1)
        unpack(t, 0, te)
        small_start(1 + t, 2, te, te)

        @pl.loop(EARLY[t], G)
        def _(g):
            big_start(t, g)

        for f in range(4 if t else 1):
            acc[f] = jnp.zeros_like(acc[f])
        small_finish(1 + t, 2, te, te)
        coefficients()

        @pl.loop(0, G)
        def _(g):
            advance(t, g)
            if t + 1 < STEPS:
                @pl.when(g < EARLY[t + 1])
                def _():
                    big_start(t + 1, g)

        if t + 1 < STEPS:
            fold([(drv, 0)])
            for y in range(Y):
                put_plane(t + 1, 0, y, drv[y, XO:XO + X, :])
            psum_start(t + 1, 1)

    fold([(te, 0), (fxe, 2), (fye, 2), (drv, 0)])
    small_start(3, 1, fxe, fye)
    small_finish(3, 1, fxe, fye)
    for y in range(Y):
        fz = drv[y, XO:XO + X, :]
        energy = te[y, XO:XO + X, :]
        spread = 0.5 * (fxe[y + 2, XO + 1:XO + 1 + X, :] - fxe[y + 2, XO - 1:XO - 1 + X, :])
        spread = spread + 0.5 * (fye[y + 3, XO:XO + X, :] - fye[y + 1, XO:XO + X, :])
        spread = spread + 0.5 * (shift_up(fz) - shift_down(fz))
        put_plane(2, 0, y, energy)
        put_plane(2, 1, y, energy - flux_weight * spread)
    psum_start(2, 2)
    psum_finish(2, 2)
    unpack(2, 0, pe)
    unpack(2, 1, fye)
    for sweep in range(SWEEPS):
        small_start(4 + sweep, 1, pe, pe)
        small_finish(4 + sweep, 1, pe, pe)
        potential = []
        for y in range(Y):
            p = pe[y + 2, XO:XO + X, :]
            k = 1.0 / (1.0 + p * p)
            weighted = diffusion_mass * fye[y + 2, XO:XO + X, :]
            weights = jnp.full_like(p, diffusion_mass)
            for n in (pe[y + 2, XO - 1:XO - 1 + X, :], pe[y + 2, XO + 1:XO + 1 + X, :],
                      pe[y + 1, XO:XO + X, :], pe[y + 3, XO:XO + X, :], shift_down(p), shift_up(p)):
                couple = 0.5 * (k + 1.0 / (1.0 + n * n))
                weighted = weighted + couple * n
                weights = weights + couple
            potential.append(weighted / weights)
        for y in range(Y):
            pe[y + 2, XO:XO + X, :] = potential[y]

    for y in range(Y):
        value = pe[y + 2, XO:XO + X, :]
        temp_out[pl.ds(y, X, stride=Y), :] = value
        cb[y + 2, XO:XO + X, :] = 2.0 * h * value / (2.0 * re[y + 2, XO:XO + X, :] + h)

    @pl.loop(0, N // U)
    def _(i):
        at = [place(i, j) for j in range(U)]
        a = [row(ca, y + 2, XO + x) for y, x in at]
        b = [row(cb, y + 2, XO + x) for y, x in at]
        for g in range(G):
            block = jnp.stack([a[j] * q2[g, at[j][0], at[j][1]] + b[j] for j in range(U)])
            out[pl.ds(g * U, U), pl.ds(pl.multiple_of(i * U, U), U), :] = jnp.swapaxes(block, 0, 1)

    for side in range(4):
        @pl.when(has[side])
        def _():
            for ev in range(4 + SWEEPS):
                small_copy(ev, 2 if ev < 3 else 1, side).wait_send()
            for t in range(2):
                @pl.loop(0, G)
                def _(g):
                    big(t, g, side, True).wait_send()
    for ev in range(3):
        for k in range(1, NO):
            psum_scatter_copy(ev, 2 if ev == 2 else 1, k).wait_send()
            psum_gather_copy(ev, 2 if ev == 2 else 1, k, mo).wait_send()


def solution(mesh):
    NO, NX, NY = (mesh.shape[name] for name in ("ord", "gx", "gy"))

    def local(distribution, relaxation):
        O, X, Y, Z = distribution.shape
        G, U, N = O // LANE_GROUP, LANE_GROUP, X * Y
        R = N // NO
        speeds = directions(lax.axis_index("ord") * O, O)
        speeds = jnp.broadcast_to(speeds.reshape(3, G, U, 1), (3, G, U, Z))
        XA = X + 16
        v = lambda *s: pltpu.VMEM(s, f32)
        dma = lambda *s: pltpu.SemaphoreType.DMA(s)
        import functools
        scratch = [
            v(G, Y, X, U, Z), v(G, Y, X, U, Z), v(G, Y, X, U, Z), v(Y + 4, X + 4, U, Z),
            v(2, 2, G, Y, 2, U, Z), v(2, 2, G, 2, X, U, Z), v(4, Y, X, U, Z), v(N, Z),
            v(Y + 4, XA, Z), v(Y + 4, XA, Z), v(Y + 4, XA, Z), v(Y + 4, XA, Z), v(Y + 4, XA, Z), v(Y + 4, XA, Z),
            v(Y, X + 8, Z), v(Y, X + 8, Z), v(Y + 1, X, Z), v(Y + 1, X, Z), v(2, Y, X, Z), v(2, Y, X, Z),
            v(Y + 4, XA, Z), v(Y + 4, XA, Z),
            v(3, NO, 2, R, Z), v(3, NO, 2, R, Z), v(3, NO, 2, R, Z),
            v(4 + SWEEPS, 2, 2, Y, Z), v(4 + SWEEPS, 2, 2, X, Z), v(4 + SWEEPS, 2, 2, Y, Z), v(4 + SWEEPS, 2, 2, X, Z),
            dma(2, G, 4), dma(2, G, 4), dma(4 + SWEEPS, 4), dma(4 + SWEEPS, 4), dma(3, 2, NO), dma(3, 2, NO),
        ]
        updated, temperature = pl.pallas_call(
            functools.partial(kernel, (NO, NX, NY, O, X, Y, Z)),
            out_shape=(jax.ShapeDtypeStruct((O, N, Z), f32), jax.ShapeDtypeStruct((N, Z), f32)),
            in_specs=[pl.BlockSpec(memory_space=pltpu.VMEM)] * 3,
            out_specs=[pl.BlockSpec(memory_space=pltpu.VMEM)] * 2,
            scratch_shapes=scratch,
            compiler_params=pltpu.CompilerParams(collective_id=0, has_side_effects=True, vmem_limit_bytes=48 * 2**20),
        )(speeds, distribution.reshape(O, N, Z), relaxation.reshape(N, Z))
        return updated.reshape(O, X, Y, Z), temperature.reshape(X, Y, Z)

    return jax.shard_map(
        local,
        mesh=mesh,
        in_specs=(P("ord", "gx", "gy", None), P("gx", "gy", None)),
        out_specs=(P("ord", "gx", "gy", None), P("gx", "gy", None)),
        check_vma=False,
    )
```
